768 devices in a mesh: replica: 48 (over x_lo, z, core), fsdp: 16 (over x_hi, y).
Axes of the slice: x: 4 (x_hi: 2, x_lo: 2; x = x_hi * 2 + x_lo), y: 8, z: 12, core: 2. Of those that a mesh axis runs over, the one named last changes fastest.
Arguments:
- hidden_in: bfloat16 [98304, 4096], P(('replica', 'fsdp')), may hold values from -60 to 60
- res_grad: bfloat16 [98304, 4096], P(('replica', 'fsdp')), may hold values from -0.59765625 to 0.59765625
- value_grad: bfloat16 [98304, 512], P(('replica', 'fsdp')), may hold values from -1.5 to 1.5
- value_weight: bfloat16 [48, 4096, 512], P('replica', 'fsdp'), may hold values from -0.09375 to 0.09375
- norm_gain: float32 [48, 4096], P('replica'), may hold values from 0.5 to 1.5
- inner_frag: float32 [48, 4096, 768], P('replica', 'fsdp'), may hold values from -6 to 6
- outer_frag: float32 [4096, 768], P('fsdp'), may hold values from -6 to 6
- momentum: float32 [4096, 768], P('fsdp'), may hold values from -3 to 3
Outputs:
- hidden_grad: bfloat16 [98304, 4096], P(('replica', 'fsdp'))
- weight_grad: bfloat16 [48, 4096, 512], P('replica', 'fsdp')
- gain_grad: float32 [48, 4096], P('replica', 'fsdp')
- new_outer: float32 [4096, 768], P('fsdp')
- new_momentum: float32 [4096, 768], P('fsdp')
The draws below stay inside these ranges and needn't reach their ends.
All inputs are finite; a program needn't handle non-finite values.
Results may differ from the reference program's by a relative error of at most 0.015.
Values may be sent and summed in bfloat16 or wider, within the bound.
No kernel may reach another device: no remote copies, remote signals or barrier semaphores. Data moves between devices by JAX's collectives and lax.ppermute only.
A program may use at most 64 MiB of HBM per device.

```python
import math
import jax
import jax.numpy as jnp
from jax import lax

D = 4096
KVW = 512
FW = 768
TOK_DEV = 128
TOKENS = 98304
N_REPLICA = 48
N_FSDP = 16


def draw_hidden_in(key, part):
    first_key = jax.random.fold_in(key, 11)
    second_key = jax.random.fold_in(key, 12)
    column_scale = jnp.exp(jax.random.uniform(second_key, (D,), jnp.float32, 0.0, math.log(10.0)))
    base_values = jnp.clip(jax.random.normal(first_key, (TOKENS, D), jnp.float32), -6.0, 6.0)
    values = base_values * column_scale
    return values.astype(jnp.bfloat16)


def level_of(rng, dims, shards, least, high):
    factor_of, own = 1.0, jax.random.fold_in(rng, 6)
    for axis_at, shards_of in shards:
        draws = jnp.exp(jax.random.uniform(jax.random.fold_in(own, axis_at), (shards_of,), jnp.float32, least / len(shards), high / len(shards)))
        factor_of = factor_of * jnp.repeat(draws, dims[axis_at] // shards_of).reshape([-1 if axis == axis_at else 1 for axis in range(len(dims))])
    return factor_of


def scatter_about(rng, shape, spread, reach, pieces=(), dtype=jnp.bfloat16):
    gain = level_of(rng, shape, pieces, -0.22, 0.18) if pieces else 1.0
    entries = jax.random.normal(rng, shape, jnp.float32) * spread * gain
    return jnp.minimum(jnp.maximum(entries, -reach), reach).astype(dtype)


def setup_inputs(seed: int = 0) -> dict:
    key_of = jax.random.split(jax.random.key(seed), 9)
    hidden_in = draw_hidden_in(jax.random.fold_in(key_of[8], 71), 0)
    res_grad = scatter_about(key_of[1], (TOKENS, D), 0.1, 0.59765625, ((0, 768),))
    value_grad = scatter_about(key_of[2], (TOKENS, KVW), 0.25, 1.5, ((0, 768),))
    value_weight = scatter_about(key_of[3], (N_REPLICA, D, KVW), D ** -0.5, 0.09375, ((0, 48), (1, 16)))
    norm_gain = jnp.clip(1.0 + 0.1 * jax.random.normal(key_of[4], (N_REPLICA, D), jnp.float32), 0.5, 1.5)
    inner_frag = scatter_about(key_of[5], (N_REPLICA, D, FW), 1.0, 6.0, ((0, 48), (1, 16)), jnp.float32)
    outer_frag = scatter_about(key_of[6], (D, FW), 1.0, 6.0, ((0, 16),), jnp.float32)
    momentum = scatter_about(key_of[7], (D, FW), 0.5, 3.0, ((0, 16),), jnp.float32)
    return {"hidden_in": hidden_in, "res_grad": res_grad, "value_grad": value_grad, "value_weight": value_weight, "norm_gain": norm_gain, "inner_frag": inner_frag, "outer_frag": outer_frag, "momentum": momentum}


def replica_backward(operands):
    hidden_rows, res_rows, value_rows, weight, scales = operands
    widened = hidden_rows.astype(jnp.float32)
    inverse = lax.rsqrt(lax.optimization_barrier(jnp.mean(widened * widened, axis=1, keepdims=True)) + 1e-05)
    unit_rows = widened * inverse
    normed = (unit_rows * scales).astype(jnp.bfloat16)
    input_grad = jnp.dot(value_rows, weight.T, preferred_element_type=jnp.float32)
    gain_grad = lax.optimization_barrier(jnp.sum(input_grad * unit_rows, axis=0))
    scaled = input_grad * scales
    projection = lax.optimization_barrier(jnp.mean(scaled * unit_rows, axis=1, keepdims=True))
    hidden_grad = (res_rows.astype(jnp.float32) + inverse * (scaled - unit_rows * projection)).astype(jnp.bfloat16)
    groups_normed = normed.reshape(N_FSDP, TOK_DEV, D)
    groups_value = value_rows.reshape(N_FSDP, TOK_DEV, KVW)

    def add_group(carry, paired):
        product = jnp.dot(paired[0].T, paired[1], preferred_element_type=jnp.float32)
        rounded = lax.optimization_barrier(product.astype(jnp.bfloat16))
        return (carry + rounded.astype(jnp.float32), None)
    weight_grad, _ = lax.scan(add_group, jnp.zeros((D, KVW), jnp.float32), (groups_normed, groups_value))
    return (hidden_grad, weight_grad.astype(jnp.bfloat16), gain_grad)

def reference(hidden_in, res_grad, value_grad, value_weight, norm_gain, inner_frag, outer_frag, momentum):
    hidden_grad, weight_grad, gain_grad = lax.map(replica_backward, (hidden_in.reshape(N_REPLICA, N_FSDP * TOK_DEV, D), res_grad.reshape(N_REPLICA, N_FSDP * TOK_DEV, D), value_grad.reshape(N_REPLICA, N_FSDP * TOK_DEV, KVW), value_weight, norm_gain))
    hidden_grad = hidden_grad.reshape(TOKENS, D)

    def add_replica(carry, frag):
        return (carry + (outer_frag - frag), None)
    summed, _ = lax.scan(add_replica, jnp.zeros((D, FW), jnp.float32), inner_frag)
    average = summed / N_REPLICA
    new_momentum = 0.9 * momentum + average
    new_outer = outer_frag - 0.7 * (average + 0.9 * new_momentum)
    return (hidden_grad, weight_grad, gain_grad, new_outer, new_momentum)
```

```python
import jax
import jax.numpy as jnp
from jax import lax
from jax.experimental import pallas as pl
from jax.experimental.pallas import tpu as pltpu
from jax.sharding import Mesh, PartitionSpec as P


AXES = ("x_lo", "z", "core", "x_hi", "y")
REPLICA = AXES[:3]
FSDP = AXES[3:]
SWAP = [(0, 1), (1, 0)]
f32, bf16 = jnp.float32, jnp.bfloat16
ROWS = 16


def whole():
    return pl.BlockSpec(memory_space=pltpu.VMEM)


def scalar():
    return pl.BlockSpec(memory_space=pltpu.SMEM)


def call(kernel, out_shape, operands, flops=0):
    outs = out_shape if isinstance(out_shape, (tuple, list)) else (out_shape,)
    moved = sum(a.size * a.dtype.itemsize for a in (*operands, *outs))
    return pl.pallas_call(
        kernel,
        out_shape=out_shape,
        in_specs=[scalar() if a.dtype == jnp.int32 else whole() for a in operands],
        out_specs=jax.tree.map(lambda _: whole(), out_shape),
        cost_estimate=pl.CostEstimate(flops=flops, bytes_accessed=moved, transcendentals=0),
    )(*operands)


def shape(dims, dtype):
    return jax.ShapeDtypeStruct(dims, dtype)


def inverse_of(rows):
    return lax.rsqrt(jnp.mean(rows * rows, axis=1, keepdims=True) + 1e-05)


def norm_kernel(upper_ref, hidden_ref, scales_ref, kept_ref, sent_ref):
    tokens, width = hidden_ref.shape
    half = width // 2
    own = pl.multiple_of(upper_ref[0] * half, half)
    other = pl.multiple_of((1 - upper_ref[0]) * half, half)

    def step(index, _):
        at = pl.ds(pl.multiple_of(index * ROWS, ROWS), ROWS)
        inverse = inverse_of(hidden_ref[at, :].astype(f32))
        for start, target in ((other, sent_ref), (own, kept_ref)):
            columns = pl.ds(start, half)
            unit = hidden_ref[at, columns].astype(f32) * inverse
            target[at, :] = (unit * scales_ref[:, columns]).astype(bf16)
        return 0

    lax.fori_loop(0, tokens // ROWS, step, 0)


def pseudo_kernel(outer_ref, inner_ref, out_ref):
    for at in range(out_ref.shape[0]):
        columns = slice(at * 128, (at + 1) * 128)
        out_ref[at] = (outer_ref[:, columns] - inner_ref[:, columns]).astype(bf16)


def block_kernel(spread_ref, out_ref):
    count = spread_ref.shape[0]
    total = spread_ref[0].astype(f32)
    for at in range(1, count):
        total += spread_ref[at].astype(f32)
    mean = (total / count).astype(bf16)
    for at in range(count):
        out_ref[at] = mean


def outer_kernel(shared_ref, outer_ref, momentum_ref, new_outer_ref, new_momentum_ref):
    for at in range(shared_ref.shape[0]):
        columns = slice(at * 128, (at + 1) * 128)
        average = shared_ref[at].astype(f32)
        new_momentum = 0.9 * momentum_ref[:, columns] + average
        new_momentum_ref[:, columns] = new_momentum
        new_outer_ref[:, columns] = outer_ref[:, columns] - 0.7 * (average + 0.9 * new_momentum)


def hidden_kernel(upper_ref, hidden_ref, res_ref, scales_ref, own_ref, other_ref, out_ref):
    tokens, width = hidden_ref.shape
    half = width // 2
    own = pl.multiple_of(upper_ref[0] * half, half)
    other = pl.multiple_of((1 - upper_ref[0]) * half, half)

    def step(index, _):
        at = pl.ds(pl.multiple_of(index * ROWS, ROWS), ROWS)
        inverse = inverse_of(hidden_ref[at, :].astype(f32))
        total = jnp.zeros((ROWS, 1), f32)
        parts = ((own, own_ref), (other, other_ref))
        for start, grad_ref in parts:
            columns = pl.ds(start, half)
            scaled = grad_ref[at, :].astype(f32) * scales_ref[:, columns]
            unit = hidden_ref[at, columns].astype(f32) * inverse
            total += jnp.sum(scaled * unit, axis=1, keepdims=True)
        projection = total / width
        for start, grad_ref in parts:
            columns = pl.ds(start, half)
            scaled = grad_ref[at, :].astype(f32) * scales_ref[:, columns]
            unit = hidden_ref[at, columns].astype(f32) * inverse
            grad = res_ref[at, columns].astype(f32) + inverse * (scaled - unit * projection)
            out_ref[at, columns] = grad.astype(bf16)
        return 0

    lax.fori_loop(0, tokens // ROWS, step, 0)


def body(
    hidden_in, res_grad, value_grad, value_weight, norm_gain, inner_frag, outer_frag, momentum
):
    upper = lax.axis_index("x_hi").reshape(1)
    own_weight = value_weight[0]
    tokens, width = hidden_in.shape
    half = width // 2
    weight_half = lax.all_gather(own_weight, "y", axis=0, tiled=True)
    partner_value = lax.ppermute(value_grad, "x_hi", SWAP)

    kept, sent = call(
        norm_kernel,
        (shape((tokens, half), bf16), shape((tokens, half), bf16)),
        (upper, hidden_in, norm_gain),
    )
    received = lax.ppermute(sent, "x_hi", SWAP)
    term = lax.dot_general(
        jnp.concatenate([kept, received], axis=0),
        jnp.concatenate([value_grad, partner_value], axis=0),
        (((0,), (0,)), ((), ())),
        preferred_element_type=f32,
    ).astype(bf16)
    weight_grad = lax.psum_scatter(term, "y", scatter_dimension=0, tiled=True)

    rows, columns = outer_frag.shape
    split = (columns // 128, rows, 128)
    pseudo_grad = call(
        pseudo_kernel, shape(split, bf16), (outer_frag, inner_frag[0])
    ).reshape(48, -1, 128)
    spread = lax.all_to_all(pseudo_grad, REPLICA, 0, 0)
    block = call(block_kernel, shape(spread.shape, bf16), (spread,))
    shared = lax.all_to_all(block, REPLICA, 0, 0)
    new_outer, new_momentum = call(
        outer_kernel,
        (shape(outer_frag.shape, f32), shape(outer_frag.shape, f32)),
        (shared.reshape(split), outer_frag, momentum),
    )

    rows_by_rows = (((1,), (1,)), ((), ()))
    partner_grad = lax.dot_general(
        partner_value, weight_half, rows_by_rows, preferred_element_type=f32
    ).astype(bf16)
    other_grad = lax.ppermute(partner_grad, "x_hi", SWAP)
    own_grad = lax.dot_general(value_grad, weight_half, rows_by_rows, preferred_element_type=f32)
    hidden_grad = call(
        hidden_kernel,
        shape(hidden_in.shape, bf16),
        (upper, hidden_in, res_grad, norm_gain, own_grad, other_grad),
    )

    count = own_weight.shape[0]
    own_scales = lax.dynamic_slice_in_dim(norm_gain[0], lax.axis_index(FSDP) * count, count, 0)
    gain_grad = (
        jnp.sum(own_weight.astype(f32) * weight_grad.astype(f32), axis=1) / own_scales
    )
    return (hidden_grad, weight_grad[None], gain_grad[None], new_outer, new_momentum)


def solution(mesh):
    grid = Mesh(mesh.devices.reshape(2, 12, 2, 2, 8), AXES)
    in_specs = (
        P(AXES, None),
        P(AXES, None),
        P(AXES, None),
        P(REPLICA, FSDP, None),
        P(REPLICA, None),
        P(REPLICA, FSDP, None),
        P(FSDP, None),
        P(FSDP, None),
    )
    out_specs = (
        P(AXES, None),
        P(REPLICA, FSDP, None),
        P(REPLICA, FSDP),
        P(FSDP, None),
        P(FSDP, None),
    )

    def step(*arrays):
        return body(*arrays)

    step = jax.shard_map(step, mesh=grid, in_specs=in_specs, out_specs=out_specs, check_vma=False)
    return step
```

```python
import jax
import jax.numpy as jnp
from jax import lax
from jax.experimental import pallas as pl
from jax.experimental.pallas import tpu as pltpu
from jax.sharding import Mesh, PartitionSpec as P


AXES = ("x_lo", "z", "core", "x_hi", "y")
REPLICA = AXES[:3]
FSDP = AXES[3:]
SWAP = [(0, 1), (1, 0)]
FORWARD = [(at, (at + 1) % 8) for at in range(8)]
BACKWARD = [(at, (at + 7) % 8) for at in range(8)]
f32, bf16 = jnp.float32, jnp.bfloat16
ROWS = 16


def whole():
    return pl.BlockSpec(memory_space=pltpu.VMEM)


def scalar():
    return pl.BlockSpec(memory_space=pltpu.SMEM)


def call(kernel, out_shape, operands, flops=0):
    outs = out_shape if isinstance(out_shape, (tuple, list)) else (out_shape,)
    moved = sum(a.size * a.dtype.itemsize for a in (*operands, *outs))
    return pl.pallas_call(
        kernel,
        out_shape=out_shape,
        in_specs=[scalar() if a.dtype == jnp.int32 else whole() for a in operands],
        out_specs=jax.tree.map(lambda _: whole(), out_shape),
        cost_estimate=pl.CostEstimate(flops=flops, bytes_accessed=moved, transcendentals=0),
    )(*operands)


def shape(dims, dtype):
    return jax.ShapeDtypeStruct(dims, dtype)


def inverse_of(rows):
    return lax.rsqrt(jnp.mean(rows * rows, axis=1, keepdims=True) + 1e-05)


def norm_kernel(upper_ref, hidden_ref, scales_ref, kept_ref, sent_ref):
    tokens, width = hidden_ref.shape
    half = width // 2
    own = pl.multiple_of(upper_ref[0] * half, half)
    other = pl.multiple_of((1 - upper_ref[0]) * half, half)

    def step(index, _):
        at = pl.ds(pl.multiple_of(index * ROWS, ROWS), ROWS)
        inverse = inverse_of(hidden_ref[at, :].astype(f32))
        for start, target in ((other, sent_ref), (own, kept_ref)):
            columns = pl.ds(start, half)
            unit = hidden_ref[at, columns].astype(f32) * inverse
            target[at, :] = (unit * scales_ref[:, columns]).astype(bf16)
        return 0

    lax.fori_loop(0, tokens // ROWS, step, 0)


def pseudo_kernel(outer_ref, inner_ref, out_ref):
    for at in range(out_ref.shape[0]):
        columns = slice(at * 128, (at + 1) * 128)
        out_ref[at] = (outer_ref[:, columns] - inner_ref[:, columns]).astype(bf16)


def block_kernel(spread_ref, out_ref):
    count = spread_ref.shape[0]
    total = spread_ref[0].astype(f32)
    for at in range(1, count):
        total += spread_ref[at].astype(f32)
    mean = (total / count).astype(bf16)
    for at in range(count):
        out_ref[at] = mean


def outer_kernel(shared_ref, outer_ref, momentum_ref, new_outer_ref, new_momentum_ref):
    for at in range(shared_ref.shape[0]):
        columns = slice(at * 128, (at + 1) * 128)
        average = shared_ref[at].astype(f32)
        new_momentum = 0.9 * momentum_ref[:, columns] + average
        new_momentum_ref[:, columns] = new_momentum
        new_outer_ref[:, columns] = outer_ref[:, columns] - 0.7 * (average + 0.9 * new_momentum)


def hidden_kernel(upper_ref, hidden_ref, res_ref, scales_ref, own_ref, other_ref, out_ref):
    tokens, width = hidden_ref.shape
    half = width // 2
    own = pl.multiple_of(upper_ref[0] * half, half)
    other = pl.multiple_of((1 - upper_ref[0]) * half, half)

    def step(index, _):
        at = pl.ds(pl.multiple_of(index * ROWS, ROWS), ROWS)
        inverse = inverse_of(hidden_ref[at, :].astype(f32))
        total = jnp.zeros((ROWS, 1), f32)
        parts = ((own, own_ref), (other, other_ref))
        for start, grad_ref in parts:
            columns = pl.ds(start, half)
            scaled = grad_ref[at, :].astype(f32) * scales_ref[:, columns]
            unit = hidden_ref[at, columns].astype(f32) * inverse
            total += jnp.sum(scaled * unit, axis=1, keepdims=True)
        projection = total / width
        for start, grad_ref in parts:
            columns = pl.ds(start, half)
            scaled = grad_ref[at, :].astype(f32) * scales_ref[:, columns]
            unit = hidden_ref[at, columns].astype(f32) * inverse
            grad = res_ref[at, columns].astype(f32) + inverse * (scaled - unit * projection)
            out_ref[at, columns] = grad.astype(bf16)
        return 0

    lax.fori_loop(0, tokens // ROWS, step, 0)


def term_kernel(place_ref, kept_ref, received_ref, value_ref, partner_ref, *out_refs):
    rows = out_refs[-1].shape[0]
    far_up, far_down, up3, down3, up2, down2, up1, down1, own = out_refs
    middle = far_up.shape[1]

    def term(step):
        columns = pl.ds(pl.multiple_of(lax.rem(place_ref[0] + step, 8) * rows, rows), rows)
        across = (((0,), (0,)), ((), ()))
        return lax.dot_general(
            kept_ref[:, columns], value_ref[...], across, preferred_element_type=f32
        ) + lax.dot_general(
            received_ref[:, columns], partner_ref[...], across, preferred_element_type=f32
        )

    far = term(4).astype(bf16)
    far_up[...] = far[:, :middle]
    far_down[...] = far[:, middle:]
    for step, target in ((3, up3), (5, down3), (2, up2), (6, down2), (1, up1), (7, down1), (0, own)):
        target[...] = term(step).astype(target.dtype)


def first_add_kernel(up_ref, down_ref, from_left_ref, from_right_ref, up_out, down_out):
    middle = from_left_ref.shape[1]
    low, high = slice(0, middle), slice(middle, 2 * middle)
    up_out[:, low] = (up_ref[:, low].astype(f32) + from_left_ref[...].astype(f32)).astype(bf16)
    up_out[:, high] = up_ref[:, high]
    down_out[:, low] = down_ref[:, low]
    down_out[:, high] = (
        down_ref[:, high].astype(f32) + from_right_ref[...].astype(f32)
    ).astype(bf16)


def add_kernel(up_ref, down_ref, from_left_ref, from_right_ref, up_out, down_out):
    up_out[...] = (up_ref[...].astype(f32) + from_left_ref[...].astype(f32)).astype(bf16)
    down_out[...] = (down_ref[...].astype(f32) + from_right_ref[...].astype(f32)).astype(bf16)


def weight_kernel(
    place_ref, own_ref, from_left_ref, from_right_ref, weight_ref, scales_ref, grad_ref, gain_ref
):
    rows = own_ref.shape[0]
    total = own_ref[...] + from_left_ref[...].astype(f32) + from_right_ref[...].astype(f32)
    grad_ref[...] = total.astype(bf16)
    products = weight_ref[...].astype(f32) * total
    sums = lax.dot_general(
        jnp.ones((8, products.shape[1]), f32),
        products,
        (((1,), (1,)), ((), ())),
        precision=lax.Precision.HIGHEST,
        preferred_element_type=f32,
    )
    columns = pl.ds(pl.multiple_of(place_ref[0] * rows, rows), rows)
    gain_ref[...] = sums[:1, :] / scales_ref[:, columns]


def body(
    hidden_in, res_grad, value_grad, value_weight, norm_gain, inner_frag, outer_frag, momentum
):
    upper = lax.axis_index("x_hi").reshape(1)
    place = lax.axis_index("y").reshape(1)
    own_weight = value_weight[0]
    tokens, width = hidden_in.shape
    half = width // 2
    weight_half = lax.all_gather(own_weight, "y", axis=0, tiled=True)
    partner_value = lax.ppermute(value_grad, "x_hi", SWAP)

    kept, sent = call(
        norm_kernel,
        (shape((tokens, half), bf16), shape((tokens, half), bf16)),
        (upper, hidden_in, norm_gain),
    )
    received = lax.ppermute(sent, "x_hi", SWAP)
    block = own_weight.shape
    narrow = (block[0], block[1] // 2)
    far_up, far_down, up3, down3, up2, down2, up1, down1, own_sum = call(
        term_kernel,
        (shape(narrow, bf16),) * 2 + (shape(block, bf16),) * 6 + (shape(block, f32),),
        (place, kept, received, value_grad, partner_value),
    )

    def hop(up, down):
        up = lax.ppermute(up, "y", FORWARD)
        down = lax.ppermute(down, "y", BACKWARD)
        return up, down

    pair = (shape(block, bf16),) * 2
    left, right = hop(far_up, far_down)
    up3, down3 = call(first_add_kernel, pair, (up3, down3, left, right))
    left, right = hop(up3, down3)
    up2, down2 = call(add_kernel, pair, (up2, down2, left, right))
    left, right = hop(up2, down2)
    up1, down1 = call(add_kernel, pair, (up1, down1, left, right))
    left, right = hop(up1, down1)
    weight_grad, gain_grad = call(
        weight_kernel,
        (shape(block, bf16), shape((1, block[0]), f32)),
        (lax.axis_index(FSDP).reshape(1), own_sum, left, right, own_weight, norm_gain),
    )

    rows, columns = outer_frag.shape
    split = (columns // 128, rows, 128)
    pseudo_grad = call(
        pseudo_kernel, shape(split, bf16), (outer_frag, inner_frag[0])
    ).reshape(48, -1, 128)
    spread = lax.all_to_all(pseudo_grad, REPLICA, 0, 0)
    block = call(block_kernel, shape(spread.shape, bf16), (spread,))
    shared = lax.all_to_all(block, REPLICA, 0, 0)
    new_outer, new_momentum = call(
        outer_kernel,
        (shape(outer_frag.shape, f32), shape(outer_frag.shape, f32)),
        (shared.reshape(split), outer_frag, momentum),
    )

    rows_by_rows = (((1,), (1,)), ((), ()))
    partner_grad = lax.dot_general(
        partner_value, weight_half, rows_by_rows, preferred_element_type=f32
    ).astype(bf16)
    other_grad = lax.ppermute(partner_grad, "x_hi", SWAP)
    own_grad = lax.dot_general(value_grad, weight_half, rows_by_rows, preferred_element_type=f32)
    hidden_grad = call(
        hidden_kernel,
        shape(hidden_in.shape, bf16),
        (upper, hidden_in, res_grad, norm_gain, own_grad, other_grad),
    )

    return (hidden_grad, weight_grad[None], gain_grad, new_outer, new_momentum)


def solution(mesh):
    grid = Mesh(mesh.devices.reshape(2, 12, 2, 2, 8), AXES)
    in_specs = (
        P(AXES, None),
        P(AXES, None),
        P(AXES, None),
        P(REPLICA, FSDP, None),
        P(REPLICA, None),
        P(REPLICA, FSDP, None),
        P(FSDP, None),
        P(FSDP, None),
    )
    out_specs = (
        P(AXES, None),
        P(REPLICA, FSDP, None),
        P(REPLICA, FSDP),
        P(FSDP, None),
        P(FSDP, None),
    )

    def step(*arrays):
        return body(*arrays)

    step = jax.shard_map(step, mesh=grid, in_specs=in_specs, out_specs=out_specs, check_vma=False)
    return step
```

```python
import jax
import jax.numpy as jnp
from jax import lax
from jax.experimental import pallas as pl
from jax.experimental.pallas import tpu as pltpu
from jax.sharding import Mesh, PartitionSpec as P


AXES = ("x_lo", "z", "core", "x_hi", "y")
REPLICA = AXES[:3]
FSDP = AXES[3:]
SWAP = [(0, 1), (1, 0)]
f32, bf16 = jnp.float32, jnp.bfloat16
ROWS = 16


def whole():
    return pl.BlockSpec(memory_space=pltpu.VMEM)


def scalar():
    return pl.BlockSpec(memory_space=pltpu.SMEM)


def call(kernel, out_shape, operands, flops=0):
    outs = out_shape if isinstance(out_shape, (tuple, list)) else (out_shape,)
    moved = sum(a.size * a.dtype.itemsize for a in (*operands, *outs))
    return pl.pallas_call(
        kernel,
        out_shape=out_shape,
        in_specs=[scalar() if a.dtype == jnp.int32 else whole() for a in operands],
        out_specs=jax.tree.map(lambda _: whole(), out_shape),
        cost_estimate=pl.CostEstimate(flops=flops, bytes_accessed=moved, transcendentals=0),
    )(*operands)


def shape(dims, dtype):
    return jax.ShapeDtypeStruct(dims, dtype)


def inverse_of(rows):
    return lax.rsqrt(jnp.mean(rows * rows, axis=1, keepdims=True) + 1e-05)


def norm_kernel(hidden_ref, scales_ref, out_ref):
    peers, tokens, width = out_ref.shape
    half, piece = peers * width // 2, width // 2

    def step(index, _):
        at = pl.ds(pl.multiple_of(index * ROWS, ROWS), ROWS)
        inverse = inverse_of(hidden_ref[at, :].astype(f32))
        for peer in range(peers):
            for side in range(2):
                columns = pl.ds(side * half + peer * piece, piece)
                unit = hidden_ref[at, columns].astype(f32) * inverse
                normed = (unit * scales_ref[:, columns]).astype(bf16)
                out_ref[peer, at, pl.ds(side * piece, piece)] = normed
        return 0

    lax.fori_loop(0, tokens // ROWS, step, 0)


def grad_kernel(upper_ref, value_ref, own_ref, other_ref, out_ref):
    piece = own_ref.shape[0]
    for side, weight_ref in ((upper_ref[0], own_ref), (1 - upper_ref[0], other_ref)):
        columns = pl.ds(pl.multiple_of(side * piece, piece), piece)
        weight = weight_ref[...]
        for peer in range(value_ref.shape[0]):
            grad = lax.dot_general(
                value_ref[peer], weight, (((1,), (1,)), ((), ())), preferred_element_type=f32
            )
            out_ref[peer, :, columns] = grad.astype(bf16)


def weight_kernel(upper_ref, normed_ref, value_ref, own_ref, sent_ref):
    piece = own_ref.shape[0]
    for side, target in ((1 - upper_ref[0], sent_ref), (upper_ref[0], own_ref)):
        columns = pl.ds(pl.multiple_of(side * piece, piece), piece)
        target[...] = lax.dot_general(
            normed_ref[:, columns],
            value_ref[...],
            (((0,), (0,)), ((), ())),
            preferred_element_type=f32,
        ).astype(target.dtype)


def quarter(place_ref, step, rows):
    core = lax.rem(place_ref[0] + step // 2, 2)
    side = lax.rem(place_ref[1] + step % 2, 2)
    return pl.ds(pl.multiple_of((core * 2 + side) * rows, rows), rows)


def pseudo_kernel(place_ref, outer_ref, inner_ref, own_ref, *sent_refs):
    rows = own_ref.shape[0]
    for step, target in enumerate((own_ref, *sent_refs)):
        at = quarter(place_ref, step, rows)
        target[...] = (outer_ref[at, :] - inner_ref[at, :]).astype(target.dtype)


def fold_kernel(own_ref, first_ref, second_ref, third_ref, out_ref):
    total = own_ref[...]
    for ref in (first_ref, second_ref, third_ref):
        total += ref[...].astype(f32)
    out_ref[...] = total.astype(bf16)


def mean_kernel(sums_ref, out_ref):
    def step(index, _):
        at = pl.ds(pl.multiple_of(index * ROWS, ROWS), ROWS)
        total = sums_ref[0, at, :].astype(f32)
        for part in range(1, sums_ref.shape[0]):
            total += sums_ref[part, at, :].astype(f32)
        out_ref[at, :] = (total / 48).astype(bf16)
        return 0

    lax.fori_loop(0, out_ref.shape[0] // ROWS, step, 0)


def outer_kernel(
    place_ref,
    own_ref,
    first_ref,
    second_ref,
    third_ref,
    outer_ref,
    momentum_ref,
    new_outer_ref,
    new_momentum_ref,
):
    for step, ref in enumerate((own_ref, first_ref, second_ref, third_ref)):
        at = quarter(place_ref, step, own_ref.shape[0])
        average = ref[...].astype(f32)
        new_momentum = 0.9 * momentum_ref[at, :] + average
        new_momentum_ref[at, :] = new_momentum
        new_outer_ref[at, :] = outer_ref[at, :] - 0.7 * (average + 0.9 * new_momentum)


def total_kernel(
    place_ref, own_ref, received_ref, weight_ref, scales_ref, grad_ref, gain_ref
):
    rows = own_ref.shape[0]
    total = own_ref[...] + received_ref[...].astype(f32)
    grad_ref[...] = total.astype(bf16)
    products = weight_ref[...].astype(f32) * total
    sums = lax.dot_general(
        jnp.ones((8, products.shape[1]), f32),
        products,
        (((1,), (1,)), ((), ())),
        precision=lax.Precision.HIGHEST,
        preferred_element_type=f32,
    )
    columns = pl.ds(pl.multiple_of(place_ref[0] * rows, rows), rows)
    gain_ref[...] = sums[:1, :] / scales_ref[:, columns]


def hidden_kernel(hidden_ref, res_ref, scales_ref, grad_ref, out_ref):
    peers, tokens, width = grad_ref.shape
    half, piece = peers * width // 2, width // 2

    def step(index, _):
        at = pl.ds(pl.multiple_of(index * ROWS, ROWS), ROWS)
        inverse = inverse_of(hidden_ref[at, :].astype(f32))

        def pieces():
            for peer in range(peers):
                for side in range(2):
                    columns = pl.ds(side * half + peer * piece, piece)
                    grad = grad_ref[peer, at, pl.ds(side * piece, piece)].astype(f32)
                    scaled = grad * scales_ref[:, columns]
                    yield columns, scaled, hidden_ref[at, columns].astype(f32) * inverse

        total = jnp.zeros((ROWS, piece), f32)
        for _, scaled, unit in pieces():
            total += scaled * unit
        projection = jnp.sum(total, axis=1, keepdims=True) / (2 * half)
        for columns, scaled, unit in pieces():
            grad = res_ref[at, columns].astype(f32) + inverse * (scaled - unit * projection)
            out_ref[at, columns] = grad.astype(bf16)
        return 0

    lax.fori_loop(0, tokens // ROWS, step, 0)


def body(
    hidden_in, res_grad, value_grad, value_weight, norm_gain, inner_frag, outer_frag, momentum
):
    upper = lax.axis_index("x_hi").reshape(1)
    own_weight = value_weight[0]
    tokens, width = hidden_in.shape
    count, features = own_weight.shape
    peers = lax.axis_size("y")
    values = lax.all_gather(value_grad, "y", axis=0)
    other_weight = lax.ppermute(own_weight, "x_hi", SWAP)

    exchange = shape((peers, tokens, width // peers), bf16)
    normed = call(norm_kernel, exchange, (hidden_in, norm_gain))
    normed = lax.all_to_all(normed, "y", 0, 0)
    grads = call(grad_kernel, exchange, (upper, values, own_weight, other_weight))
    grads = lax.all_to_all(grads, "y", 0, 0)
    own_sum, sent_sum = call(
        weight_kernel,
        (shape((count, features), f32), shape((count, features), bf16)),
        (
            upper,
            normed.reshape(peers * tokens, -1),
            values.reshape(peers * tokens, features),
        ),
    )
    received = lax.ppermute(sent_sum, "x_hi", SWAP)

    rows, columns = outer_frag.shape
    piece = (rows // 4, columns)
    place = jnp.stack([lax.axis_index("core"), lax.axis_index("x_lo")])

    def trade(parts):
        received = []
        for step, part in zip((1, 2, 3), parts):
            table = [(at, at ^ (step // 2 + step % 2 * 2)) for at in range(4)]
            received.append(lax.ppermute(part, ("x_lo", "core"), table))
        return received

    own_part, *sent_parts = call(
        pseudo_kernel,
        (shape(piece, f32),) + (shape(piece, bf16),) * 3,
        (place, outer_frag, inner_frag[0]),
    )
    received_parts = trade(sent_parts)
    part = call(fold_kernel, shape(piece, bf16), (own_part, *received_parts))
    parts = lax.all_gather(part, "z", axis=0)
    mean = call(mean_kernel, shape(piece, bf16), (parts,))
    means = trade((mean,) * 3)
    new_outer, new_momentum = call(
        outer_kernel,
        (shape(outer_frag.shape, f32), shape(outer_frag.shape, f32)),
        (place, mean, *means, outer_frag, momentum),
    )
    weight_grad, gain_grad = call(
        total_kernel,
        (shape((count, features), bf16), shape((1, count), f32)),
        (lax.axis_index(FSDP).reshape(1), own_sum, received, own_weight, norm_gain),
    )

    hidden_grad = call(
        hidden_kernel, shape(hidden_in.shape, bf16), (hidden_in, res_grad, norm_gain, grads)
    )
    return (hidden_grad, weight_grad[None], gain_grad, new_outer, new_momentum)


def solution(mesh):
    grid = Mesh(mesh.devices.reshape(2, 12, 2, 2, 8), AXES)
    in_specs = (
        P(AXES, None),
        P(AXES, None),
        P(AXES, None),
        P(REPLICA, FSDP, None),
        P(REPLICA, None),
        P(REPLICA, FSDP, None),
        P(FSDP, None),
        P(FSDP, None),
    )
    out_specs = (
        P(AXES, None),
        P(REPLICA, FSDP, None),
        P(REPLICA, FSDP),
        P(FSDP, None),
        P(FSDP, None),
    )

    def step(*arrays):
        return body(*arrays)

    step = jax.shard_map(step, mesh=grid, in_specs=in_specs, out_specs=out_specs, check_vma=False)
    return step
```

```python
import jax
import jax.numpy as jnp
from jax import lax
from jax.experimental import pallas as pl
from jax.experimental.pallas import tpu as pltpu
from jax.sharding import Mesh, PartitionSpec as P


AXES = ("x_lo", "z", "core", "x_hi", "y_hi", "y_lo")
REPLICA = AXES[:3]
FSDP = AXES[3:]
GROUP = ("x_hi", "y_lo")
f32, bf16 = jnp.float32, jnp.bfloat16
ROWS = 16


def whole():
    return pl.BlockSpec(memory_space=pltpu.VMEM)


def scalar():
    return pl.BlockSpec(memory_space=pltpu.SMEM)


def call(kernel, out_shape, operands, flops=0):
    outs = out_shape if isinstance(out_shape, (tuple, list)) else (out_shape,)
    moved = sum(a.size * a.dtype.itemsize for a in (*operands, *outs))
    return pl.pallas_call(
        kernel,
        out_shape=out_shape,
        in_specs=[scalar() if a.dtype == jnp.int32 else whole() for a in operands],
        out_specs=jax.tree.map(lambda _: whole(), out_shape),
        cost_estimate=pl.CostEstimate(flops=flops, bytes_accessed=moved, transcendentals=0),
    )(*operands)


def shape(dims, dtype):
    return jax.ShapeDtypeStruct(dims, dtype)


def inverse_of(rows):
    return lax.rsqrt(jnp.mean(rows * rows, axis=1, keepdims=True) + 1e-05)


PIECE = 256


def pieces(group_ref, step):
    member = lax.bitwise_xor(group_ref[0], step)
    start = lax.shift_right_logical(member, 1) * 2048 + lax.bitwise_and(member, 1) * PIECE
    return [pl.ds(pl.multiple_of(start + at * 2 * PIECE, PIECE), PIECE) for at in range(4)]


def norm_kernel(group_ref, hidden_ref, value_ref, scales_ref, *out_refs):
    def step(index, _):
        at = pl.ds(pl.multiple_of(index * ROWS, ROWS), ROWS)
        inverse = inverse_of(hidden_ref[at, :].astype(f32))
        for away in (1, 2, 3, 0):
            for place, columns in enumerate(pieces(group_ref, away)):
                unit = hidden_ref[at, columns].astype(f32) * inverse
                normed = (unit * scales_ref[:, columns]).astype(bf16)
                out_refs[away][at, pl.ds(place * PIECE, PIECE)] = normed
        return 0

    lax.fori_loop(0, hidden_ref.shape[0] // ROWS, step, 0)
    for ref in out_refs[1:]:
        ref[:, 4 * PIECE :] = value_ref[...]


def term_kernel(kept_ref, value_ref, first_ref, second_ref, third_ref, out_ref):
    across = (((0,), (0,)), ((), ()))
    for at in range(4):
        columns = slice(at * PIECE, (at + 1) * PIECE)
        total = lax.dot_general(
            kept_ref[:, columns], value_ref[...], across, preferred_element_type=f32
        )
        for ref in (first_ref, second_ref, third_ref):
            total += lax.dot_general(
                ref[:, columns], ref[:, 4 * PIECE :], across, preferred_element_type=f32
            )
        out_ref[columns, :] = total.astype(bf16)


def grad_kernel(weight_ref, first_ref, second_ref, third_ref, *out_refs):
    weight = weight_ref[...]
    for ref, out_ref in zip((first_ref, second_ref, third_ref), out_refs):
        out_ref[...] = lax.dot_general(
            ref[:, 4 * PIECE :], weight, (((1,), (1,)), ((), ())), preferred_element_type=f32
        ).astype(bf16)


def gain_kernel(place_ref, grad_ref, weight_ref, scales_ref, gain_ref):
    rows = grad_ref.shape[0]
    products = weight_ref[...].astype(f32) * grad_ref[...].astype(f32)
    sums = lax.dot_general(
        jnp.ones((8, products.shape[1]), f32),
        products,
        (((1,), (1,)), ((), ())),
        precision=lax.Precision.HIGHEST,
        preferred_element_type=f32,
    )
    columns = pl.ds(pl.multiple_of(place_ref[0] * rows, rows), rows)
    gain_ref[...] = sums[:1, :] / scales_ref[:, columns]


def pseudo_kernel(outer_ref, inner_ref, out_ref):
    for at in range(out_ref.shape[0]):
        columns = slice(at * 128, (at + 1) * 128)
        out_ref[at] = (outer_ref[:, columns] - inner_ref[:, columns]).astype(bf16)


def block_kernel(spread_ref, out_ref):
    count = spread_ref.shape[0]
    total = spread_ref[0].astype(f32)
    for at in range(1, count):
        total += spread_ref[at].astype(f32)
    mean = (total / count).astype(bf16)
    for at in range(count):
        out_ref[at] = mean


def outer_kernel(shared_ref, outer_ref, momentum_ref, new_outer_ref, new_momentum_ref):
    for at in range(shared_ref.shape[0]):
        columns = slice(at * 128, (at + 1) * 128)
        average = shared_ref[at].astype(f32)
        new_momentum = 0.9 * momentum_ref[:, columns] + average
        new_momentum_ref[:, columns] = new_momentum
        new_outer_ref[:, columns] = outer_ref[:, columns] - 0.7 * (average + 0.9 * new_momentum)


def hidden_kernel(
    group_ref, hidden_ref, res_ref, scales_ref, own_ref, first_ref, second_ref, third_ref, out_ref
):
    def step(index, _):
        at = pl.ds(pl.multiple_of(index * ROWS, ROWS), ROWS)
        inverse = inverse_of(hidden_ref[at, :].astype(f32))

        def parts():
            for away, ref in enumerate((own_ref, first_ref, second_ref, third_ref)):
                for place, columns in enumerate(pieces(group_ref, away)):
                    grad = ref[at, pl.ds(place * PIECE, PIECE)].astype(f32)
                    scaled = grad * scales_ref[:, columns]
                    yield columns, scaled, hidden_ref[at, columns].astype(f32) * inverse

        total = jnp.zeros((ROWS, PIECE), f32)
        for _, scaled, unit in parts():
            total += scaled * unit
        projection = jnp.sum(total, axis=1, keepdims=True) / hidden_ref.shape[1]
        for columns, scaled, unit in parts():
            grad = res_ref[at, columns].astype(f32) + inverse * (scaled - unit * projection)
            out_ref[at, columns] = grad.astype(bf16)
        return 0

    lax.fori_loop(0, hidden_ref.shape[0] // ROWS, step, 0)


def body(
    hidden_in, res_grad, value_grad, value_weight, norm_gain, inner_frag, outer_frag, momentum
):
    group = lax.axis_index(GROUP).reshape(1)
    own_weight = value_weight[0]
    tokens, width = hidden_in.shape
    features = value_grad.shape[1]
    quarter = width // 4
    weights = lax.all_gather(own_weight, "y_hi", axis=0, tiled=True)

    def trade(parts):
        received = []
        for step, part in enumerate(parts, 1):
            table = [(at, at ^ step) for at in range(4)]
            received.append(lax.ppermute(part, GROUP, table))
        return received

    kept, *sent = call(
        norm_kernel,
        (shape((tokens, quarter), bf16),) + (shape((tokens, quarter + features), bf16),) * 3,
        (group, hidden_in, value_grad, norm_gain),
    )
    received = trade(sent)
    term = call(term_kernel, shape((quarter, features), bf16), (kept, value_grad, *received))
    weight_grad = lax.psum_scatter(term, "y_hi", scatter_dimension=0, tiled=True)

    rows, columns = outer_frag.shape
    split = (columns // 128, rows, 128)
    pseudo_grad = call(
        pseudo_kernel, shape(split, bf16), (outer_frag, inner_frag[0])
    ).reshape(48, -1, 128)
    spread = lax.all_to_all(pseudo_grad, REPLICA, 0, 0)
    block = call(block_kernel, shape(spread.shape, bf16), (spread,))
    shared = lax.all_to_all(block, REPLICA, 0, 0)
    new_outer, new_momentum = call(
        outer_kernel,
        (shape(outer_frag.shape, f32), shape(outer_frag.shape, f32)),
        (shared.reshape(split), outer_frag, momentum),
    )

    grads = call(grad_kernel, (shape((tokens, quarter), bf16),) * 3, (weights, *received))
    grads = trade(grads)
    own_grad = lax.dot_general(
        value_grad, weights, (((1,), (1,)), ((), ())), preferred_element_type=f32
    )
    hidden_grad = call(
        hidden_kernel,
        shape(hidden_in.shape, bf16),
        (group, hidden_in, res_grad, norm_gain, own_grad, *grads),
    )
    gain_grad = call(
        gain_kernel,
        shape((1, own_weight.shape[0]), f32),
        (lax.axis_index(FSDP).reshape(1), weight_grad, own_weight, norm_gain),
    )
    return (hidden_grad, weight_grad[None], gain_grad, new_outer, new_momentum)


def solution(mesh):
    grid = Mesh(mesh.devices.reshape(2, 12, 2, 2, 4, 2), AXES)
    in_specs = (
        P(AXES, None),
        P(AXES, None),
        P(AXES, None),
        P(REPLICA, FSDP, None),
        P(REPLICA, None),
        P(REPLICA, FSDP, None),
        P(FSDP, None),
        P(FSDP, None),
    )
    out_specs = (
        P(AXES, None),
        P(REPLICA, FSDP, None),
        P(REPLICA, FSDP),
        P(FSDP, None),
        P(FSDP, None),
    )

    def step(*arrays):
        return body(*arrays)

    step = jax.shard_map(step, mesh=grid, in_specs=in_specs, out_specs=out_specs, check_vma=False)
    return step
```

```python
import jax
import jax.numpy as jnp
from jax import lax
from jax.experimental import pallas as pl
from jax.experimental.pallas import tpu as pltpu
from jax.sharding import Mesh, PartitionSpec as P


AXES = ("x_lo", "z", "core", "x_hi", "y_hi", "y_lo")
REPLICA = AXES[:3]
FSDP = AXES[3:]
SWAP = [(0, 1), (1, 0)]
f32, bf16 = jnp.float32, jnp.bfloat16
ROWS = 16


def whole():
    return pl.BlockSpec(memory_space=pltpu.VMEM)


def scalar():
    return pl.BlockSpec(memory_space=pltpu.SMEM)


def call(kernel, out_shape, operands, flops=0):
    outs = out_shape if isinstance(out_shape, (tuple, list)) else (out_shape,)
    moved = sum(a.size * a.dtype.itemsize for a in (*operands, *outs))
    return pl.pallas_call(
        kernel,
        out_shape=out_shape,
        in_specs=[scalar() if a.dtype == jnp.int32 else whole() for a in operands],
        out_specs=jax.tree.map(lambda _: whole(), out_shape),
        cost_estimate=pl.CostEstimate(flops=flops, bytes_accessed=moved, transcendentals=0),
    )(*operands)


def shape(dims, dtype):
    return jax.ShapeDtypeStruct(dims, dtype)


def inverse_of(rows):
    return lax.rsqrt(jnp.mean(rows * rows, axis=1, keepdims=True) + 1e-05)


def pair_kernel(parity_ref, own_ref, other_ref, out_ref):
    out_ref[parity_ref[0]] = own_ref[...]
    out_ref[1 - parity_ref[0]] = other_ref[...]


def sides(upper_ref, half):
    return [
        pl.ds(pl.multiple_of(side * half, half), half) for side in (upper_ref[0], 1 - upper_ref[0])
    ]


def norm_kernel(upper_ref, hidden_ref, scales_ref, kept_ref, sent_ref, inverse_ref):
    tokens, width = hidden_ref.shape
    own, other = sides(upper_ref, width // 2)

    def step(index, _):
        at = pl.ds(pl.multiple_of(index * ROWS, ROWS), ROWS)
        inverse = inverse_of(hidden_ref[at, :].astype(f32))
        inverse_ref[at, :] = jnp.broadcast_to(inverse, (ROWS, 128))
        for columns, target in ((other, sent_ref), (own, kept_ref)):
            unit = hidden_ref[at, columns].astype(f32) * inverse
            target[at, :] = (unit * scales_ref[:, columns]).astype(bf16)
        return 0

    lax.fori_loop(0, tokens // ROWS, step, 0, unroll=2)


def pseudo_kernel(outer_ref, inner_ref, out_ref):
    for at in range(out_ref.shape[0]):
        columns = slice(at * 128, (at + 1) * 128)
        out_ref[at] = (outer_ref[:, columns] - inner_ref[:, columns]).astype(bf16)


def block_kernel(spread_ref, out_ref):
    count = spread_ref.shape[0]
    total = spread_ref[0].astype(f32)
    for at in range(1, count):
        total += spread_ref[at].astype(f32)
    mean = (total / count).astype(bf16)
    for at in range(count):
        out_ref[at] = mean


def outer_kernel(shared_ref, outer_ref, momentum_ref, new_outer_ref, new_momentum_ref):
    for at in range(shared_ref.shape[0]):
        columns = slice(at * 128, (at + 1) * 128)
        average = shared_ref[at].astype(f32)
        new_momentum = 0.9 * momentum_ref[:, columns] + average
        new_momentum_ref[:, columns] = new_momentum
        new_outer_ref[:, columns] = outer_ref[:, columns] - 0.7 * (average + 0.9 * new_momentum)


def hidden_kernel(
    upper_ref, hidden_ref, res_ref, scales_ref, inverse_ref, own_ref, other_ref, out_ref
):
    tokens, width = hidden_ref.shape
    parts = tuple(zip(sides(upper_ref, width // 2), (own_ref, other_ref)))

    def step(index, _):
        at = pl.ds(pl.multiple_of(index * ROWS, ROWS), ROWS)
        inverse = inverse_ref[at, :][:, :1]
        total = jnp.zeros((ROWS, 1), f32)
        for columns, grad_ref in parts:
            scaled = grad_ref[at, :].astype(f32) * scales_ref[:, columns]
            total += jnp.sum(scaled * hidden_ref[at, columns].astype(f32), axis=1, keepdims=True)
        shift = inverse * (inverse * total / width)
        for columns, grad_ref in parts:
            scaled = grad_ref[at, :].astype(f32) * scales_ref[:, columns]
            inner = scaled - hidden_ref[at, columns].astype(f32) * shift
            out_ref[at, columns] = (res_ref[at, columns].astype(f32) + inverse * inner).astype(bf16)
        return 0

    lax.fori_loop(0, tokens // ROWS, step, 0, unroll=2)


def gain_kernel(place_ref, grad_ref, weight_ref, scales_ref, gain_ref):
    rows = grad_ref.shape[0]
    products = weight_ref[...].astype(f32) * grad_ref[...].astype(f32)
    sums = lax.dot_general(
        jnp.ones((8, products.shape[1]), f32),
        products,
        (((1,), (1,)), ((), ())),
        precision=lax.Precision.HIGHEST,
        preferred_element_type=f32,
    )
    columns = pl.ds(pl.multiple_of(place_ref[0] * rows, rows), rows)
    gain_ref[...] = sums[:1, :] / scales_ref[:, columns]


def body(
    hidden_in, res_grad, value_grad, value_weight, norm_gain, inner_frag, outer_frag, momentum
):
    upper = lax.axis_index("x_hi").reshape(1)
    own_weight = value_weight[0]
    tokens, width = hidden_in.shape
    half = width // 2
    other_weight = lax.ppermute(own_weight, "y_lo", SWAP)
    parity = lax.axis_index("y_lo").reshape(1)
    weight_pair = call(
        pair_kernel, shape((2, *own_weight.shape), bf16), (parity, own_weight, other_weight)
    ).reshape(-1, own_weight.shape[1])
    weight_half = lax.all_gather(weight_pair, "y_hi", axis=0, tiled=True)
    partner_value = lax.ppermute(value_grad, "x_hi", SWAP)

    kept, sent, inverse = call(
        norm_kernel,
        (
            shape((tokens, half), bf16),
            shape((tokens, half), bf16),
            shape((tokens, 128), f32),
        ),
        (upper, hidden_in, norm_gain),
    )
    received = lax.ppermute(sent, "x_hi", SWAP)
    term = lax.dot_general(
        jnp.concatenate([kept, received], axis=0),
        jnp.concatenate([value_grad, partner_value], axis=0),
        (((0,), (0,)), ((), ())),
        preferred_element_type=f32,
    ).astype(bf16)
    weight_grad = lax.psum_scatter(
        term, ("y_hi", "y_lo"), scatter_dimension=0, tiled=True
    )

    rows, columns = outer_frag.shape
    split = (columns // 128, rows, 128)
    pseudo_grad = call(
        pseudo_kernel, shape(split, bf16), (outer_frag, inner_frag[0])
    ).reshape(48, -1, 128)
    spread = lax.all_to_all(pseudo_grad, REPLICA, 0, 0)
    block = call(block_kernel, shape(spread.shape, bf16), (spread,))
    shared = lax.all_to_all(block, REPLICA, 0, 0)
    new_outer, new_momentum = call(
        outer_kernel,
        (shape(outer_frag.shape, f32), shape(outer_frag.shape, f32)),
        (shared.reshape(split), outer_frag, momentum),
    )

    rows_by_rows = (((1,), (1,)), ((), ()))
    partner_grad = lax.dot_general(
        partner_value, weight_half, rows_by_rows, preferred_element_type=f32
    ).astype(bf16)
    other_grad = lax.ppermute(partner_grad, "x_hi", SWAP)
    own_grad = lax.dot_general(value_grad, weight_half, rows_by_rows, preferred_element_type=f32)
    hidden_grad = call(
        hidden_kernel,
        shape(hidden_in.shape, bf16),
        (upper, hidden_in, res_grad, norm_gain, inverse, own_grad, other_grad),
    )

    gain_grad = call(
        gain_kernel,
        shape((1, own_weight.shape[0]), f32),
        (lax.axis_index(FSDP).reshape(1), weight_grad, own_weight, norm_gain),
    )
    return (hidden_grad, weight_grad[None], gain_grad, new_outer, new_momentum)


def solution(mesh):
    grid = Mesh(mesh.devices.reshape(2, 12, 2, 2, 4, 2), AXES)
    in_specs = (
        P(AXES, None),
        P(AXES, None),
        P(AXES, None),
        P(REPLICA, FSDP, None),
        P(REPLICA, None),
        P(REPLICA, FSDP, None),
        P(FSDP, None),
        P(FSDP, None),
    )
    out_specs = (
        P(AXES, None),
        P(REPLICA, FSDP, None),
        P(REPLICA, FSDP),
        P(FSDP, None),
        P(FSDP, None),
    )

    def step(*arrays):
        return body(*arrays)

    step = jax.shard_map(step, mesh=grid, in_specs=in_specs, out_specs=out_specs, check_vma=False)
    return step
```

```python
import jax
import jax.numpy as jnp
from jax import lax
from jax.experimental import pallas as pl
from jax.experimental.pallas import tpu as pltpu
from jax.sharding import Mesh, PartitionSpec as P


AXES = ("x_lo", "z", "core", "x_hi", "y_hi", "y_lo")
REPLICA = AXES[:3]
FSDP = AXES[3:]
SWAP = [(0, 1), (1, 0)]
TWISTED = [[0, 1, 2, 3, 12, 13, 14, 15], [8, 9, 10, 11, 4, 5, 6, 7]]
f32, bf16 = jnp.float32, jnp.bfloat16
ROWS = 16


def whole():
    return pl.BlockSpec(memory_space=pltpu.VMEM)


def scalar():
    return pl.BlockSpec(memory_space=pltpu.SMEM)


def call(kernel, out_shape, operands, flops=0):
    outs = out_shape if isinstance(out_shape, (tuple, list)) else (out_shape,)
    moved = sum(a.size * a.dtype.itemsize for a in (*operands, *outs))
    return pl.pallas_call(
        kernel,
        out_shape=out_shape,
        in_specs=[scalar() if a.dtype == jnp.int32 else whole() for a in operands],
        out_specs=jax.tree.map(lambda _: whole(), out_shape),
        cost_estimate=pl.CostEstimate(flops=flops, bytes_accessed=moved, transcendentals=0),
    )(*operands)


def shape(dims, dtype):
    return jax.ShapeDtypeStruct(dims, dtype)


def inverse_of(rows):
    return lax.rsqrt(jnp.mean(rows * rows, axis=1, keepdims=True) + 1e-05)


def sides(upper_ref, half):
    return [
        pl.ds(pl.multiple_of(side * half, half), half) for side in (upper_ref[0], 1 - upper_ref[0])
    ]


def norm_kernel(twist_ref, hidden_ref, scales_ref, kept_ref, sent_ref, inverse_ref):
    tokens, width = hidden_ref.shape
    part = width // 4
    pieces = []
    for target, side in ((sent_ref, 1 - twist_ref[0]), (kept_ref, twist_ref[0])):
        pieces.append((target, 0, pl.multiple_of(side * 2 * part, part)))
        pieces.append((target, part, pl.multiple_of((1 - side) * 2 * part + part, part)))

    def step(index, _):
        at = pl.ds(pl.multiple_of(index * ROWS, ROWS), ROWS)
        inverse = inverse_of(hidden_ref[at, :].astype(f32))
        inverse_ref[at, :] = jnp.broadcast_to(inverse, (ROWS, 128))
        for target, place, start in pieces:
            columns = pl.ds(start, part)
            unit = hidden_ref[at, columns].astype(f32) * inverse
            normed = (unit * scales_ref[:, columns]).astype(bf16)
            target[at, pl.ds(place, part)] = normed
        return 0

    lax.fori_loop(0, tokens // ROWS, step, 0, unroll=2)


def pseudo_kernel(outer_ref, inner_ref, out_ref):
    for at in range(out_ref.shape[0]):
        columns = slice(at * 128, (at + 1) * 128)
        out_ref[at] = (outer_ref[:, columns] - inner_ref[:, columns]).astype(bf16)


def block_kernel(spread_ref, out_ref):
    count = spread_ref.shape[0]
    total = spread_ref[0].astype(f32)
    for at in range(1, count):
        total += spread_ref[at].astype(f32)
    mean = (total / count).astype(bf16)
    for at in range(count):
        out_ref[at] = mean


def outer_kernel(shared_ref, outer_ref, momentum_ref, new_outer_ref, new_momentum_ref):
    for at in range(shared_ref.shape[0]):
        columns = slice(at * 128, (at + 1) * 128)
        average = shared_ref[at].astype(f32)
        new_momentum = 0.9 * momentum_ref[:, columns] + average
        new_momentum_ref[:, columns] = new_momentum
        new_outer_ref[:, columns] = outer_ref[:, columns] - 0.7 * (average + 0.9 * new_momentum)


def hidden_kernel(
    upper_ref, hidden_ref, res_ref, scales_ref, inverse_ref, own_ref, other_ref, out_ref
):
    tokens, width = hidden_ref.shape
    parts = tuple(zip(sides(upper_ref, width // 2), (own_ref, other_ref)))

    def step(index, _):
        at = pl.ds(pl.multiple_of(index * ROWS, ROWS), ROWS)
        inverse = inverse_ref[at, :][:, :1]
        total = jnp.zeros((ROWS, 1), f32)
        for columns, grad_ref in parts:
            scaled = grad_ref[at, :].astype(f32) * scales_ref[:, columns]
            total += jnp.sum(scaled * hidden_ref[at, columns].astype(f32), axis=1, keepdims=True)
        shift = inverse * (inverse * total / width)
        for columns, grad_ref in parts:
            scaled = grad_ref[at, :].astype(f32) * scales_ref[:, columns]
            inner = scaled - hidden_ref[at, columns].astype(f32) * shift
            out_ref[at, columns] = (res_ref[at, columns].astype(f32) + inverse * inner).astype(bf16)
        return 0

    lax.fori_loop(0, tokens // ROWS, step, 0, unroll=2)


def gain_kernel(place_ref, grad_ref, weight_ref, scales_ref, gain_ref):
    rows = grad_ref.shape[0]
    products = weight_ref[...].astype(f32) * grad_ref[...].astype(f32)
    sums = lax.dot_general(
        jnp.ones((8, products.shape[1]), f32),
        products,
        (((1,), (1,)), ((), ())),
        precision=lax.Precision.HIGHEST,
        preferred_element_type=f32,
    )
    columns = pl.ds(pl.multiple_of(place_ref[0] * rows, rows), rows)
    gain_ref[...] = sums[:1, :] / scales_ref[:, columns]


def body(
    hidden_in, res_grad, value_grad, value_weight, norm_gain, inner_frag, outer_frag, momentum
):
    upper = lax.axis_index("x_hi").reshape(1)
    twist = lax.bitwise_xor(lax.axis_index("x_hi"), lax.axis_index("y_hi") // 2).reshape(1)
    own_weight = value_weight[0]
    tokens, width = hidden_in.shape
    half = width // 2
    weight_half = lax.all_gather(own_weight, ("y_hi", "y_lo"), axis=0, tiled=True)
    partner_value = lax.ppermute(value_grad, "x_hi", SWAP)

    kept, sent, inverse = call(
        norm_kernel,
        (
            shape((tokens, half), bf16),
            shape((tokens, half), bf16),
            shape((tokens, 128), f32),
        ),
        (twist, hidden_in, norm_gain),
    )
    received = lax.ppermute(sent, "x_hi", SWAP)
    term = lax.dot_general(
        jnp.concatenate([kept, received], axis=0),
        jnp.concatenate([value_grad, partner_value], axis=0),
        (((0,), (0,)), ((), ())),
        preferred_element_type=f32,
    ).astype(bf16)
    weight_grad = lax.psum_scatter(
        term, FSDP, scatter_dimension=0, tiled=True, axis_index_groups=TWISTED
    )

    rows, columns = outer_frag.shape
    split = (columns // 128, rows, 128)
    pseudo_grad = call(
        pseudo_kernel, shape(split, bf16), (outer_frag, inner_frag[0])
    ).reshape(48, -1, 128)
    spread = lax.all_to_all(pseudo_grad, REPLICA, 0, 0)
    block = call(block_kernel, shape(spread.shape, bf16), (spread,))
    shared = lax.all_to_all(block, REPLICA, 0, 0)
    new_outer, new_momentum = call(
        outer_kernel,
        (shape(outer_frag.shape, f32), shape(outer_frag.shape, f32)),
        (shared.reshape(split), outer_frag, momentum),
    )

    rows_by_rows = (((1,), (1,)), ((), ()))
    partner_grad = lax.dot_general(
        partner_value, weight_half, rows_by_rows, preferred_element_type=f32
    ).astype(bf16)
    other_grad = lax.ppermute(partner_grad, "x_hi", SWAP)
    own_grad = lax.dot_general(value_grad, weight_half, rows_by_rows, preferred_element_type=f32)
    hidden_grad = call(
        hidden_kernel,
        shape(hidden_in.shape, bf16),
        (upper, hidden_in, res_grad, norm_gain, inverse, own_grad, other_grad),
    )

    gain_grad = call(
        gain_kernel,
        shape((1, own_weight.shape[0]), f32),
        (lax.axis_index(FSDP).reshape(1), weight_grad, own_weight, norm_gain),
    )
    return (hidden_grad, weight_grad[None], gain_grad, new_outer, new_momentum)


def solution(mesh):
    grid = Mesh(mesh.devices.reshape(2, 12, 2, 2, 4, 2), AXES)
    in_specs = (
        P(AXES, None),
        P(AXES, None),
        P(AXES, None),
        P(REPLICA, FSDP, None),
        P(REPLICA, None),
        P(REPLICA, FSDP, None),
        P(FSDP, None),
        P(FSDP, None),
    )
    out_specs = (
        P(AXES, None),
        P(REPLICA, FSDP, None),
        P(REPLICA, FSDP),
        P(FSDP, None),
        P(FSDP, None),
    )

    def step(*arrays):
        return body(*arrays)

    step = jax.shard_map(step, mesh=grid, in_specs=in_specs, out_specs=out_specs, check_vma=False)
    return step
```

```python
import jax
import jax.numpy as jnp
from jax import lax
from jax.experimental import pallas as pl
from jax.experimental.pallas import tpu as pltpu
from jax.sharding import Mesh, PartitionSpec as P


AXES = ("x_lo", "z", "core", "x_hi", "y_hi", "y_lo")
REPLICA = AXES[:3]
FSDP = AXES[3:]
SWAP = [(0, 1), (1, 0)]
TWISTED = [[0, 1, 2, 3, 12, 13, 14, 15], [8, 9, 10, 11, 4, 5, 6, 7]]
f32, bf16 = jnp.float32, jnp.bfloat16
ROWS = 16


def whole():
    return pl.BlockSpec(memory_space=pltpu.VMEM)


def scalar():
    return pl.BlockSpec(memory_space=pltpu.SMEM)


def call(kernel, out_shape, operands, flops=0):
    outs = out_shape if isinstance(out_shape, (tuple, list)) else (out_shape,)
    moved = sum(a.size * a.dtype.itemsize for a in (*operands, *outs))
    return pl.pallas_call(
        kernel,
        out_shape=out_shape,
        in_specs=[scalar() if a.dtype == jnp.int32 else whole() for a in operands],
        out_specs=jax.tree.map(lambda _: whole(), out_shape),
        cost_estimate=pl.CostEstimate(flops=flops, bytes_accessed=moved, transcendentals=0),
    )(*operands)


def shape(dims, dtype):
    return jax.ShapeDtypeStruct(dims, dtype)


def inverse_of(rows):
    return lax.rsqrt(jnp.mean(rows * rows, axis=1, keepdims=True) + 1e-05)


def sides(upper_ref, half):
    return [
        pl.ds(pl.multiple_of(side * half, half), half) for side in (upper_ref[0], 1 - upper_ref[0])
    ]


def norm_kernel(upper_ref, hidden_ref, scales_ref, kept_ref, sent_ref, inverse_ref):
    tokens, width = hidden_ref.shape
    own, other = sides(upper_ref, width // 2)

    def step(index, _):
        at = pl.ds(pl.multiple_of(index * ROWS, ROWS), ROWS)
        inverse = inverse_of(hidden_ref[at, :].astype(f32))
        inverse_ref[at, :] = jnp.broadcast_to(inverse, (ROWS, 128))
        for columns, target in ((other, sent_ref), (own, kept_ref)):
            unit = hidden_ref[at, columns].astype(f32) * inverse
            target[at, :] = (unit * scales_ref[:, columns]).astype(bf16)
        return 0

    lax.fori_loop(0, tokens // ROWS, step, 0, unroll=2)


def pseudo_kernel(outer_ref, inner_ref, out_ref):
    for at in range(out_ref.shape[0]):
        columns = slice(at * 128, (at + 1) * 128)
        out_ref[at] = (outer_ref[:, columns] - inner_ref[:, columns]).astype(bf16)


def block_kernel(spread_ref, out_ref):
    count = spread_ref.shape[0]
    total = spread_ref[0].astype(f32)
    for at in range(1, count):
        total += spread_ref[at].astype(f32)
    mean = (total / count).astype(bf16)
    for at in range(count):
        out_ref[at] = mean


def outer_kernel(shared_ref, outer_ref, momentum_ref, new_outer_ref, new_momentum_ref):
    for at in range(shared_ref.shape[0]):
        columns = slice(at * 128, (at + 1) * 128)
        average = shared_ref[at].astype(f32)
        new_momentum = 0.9 * momentum_ref[:, columns] + average
        new_momentum_ref[:, columns] = new_momentum
        new_outer_ref[:, columns] = outer_ref[:, columns] - 0.7 * (average + 0.9 * new_momentum)


def hidden_kernel(
    twist_ref, hidden_ref, res_ref, scales_ref, inverse_ref, own_ref, other_ref, out_ref
):
    tokens, width = hidden_ref.shape
    part = width // 4
    parts = []
    for grad_ref, side in ((own_ref, twist_ref[0]), (other_ref, 1 - twist_ref[0])):
        starts = (side * 2 * part, (1 - side) * 2 * part + part)
        for place, start in enumerate(starts):
            columns = pl.ds(pl.multiple_of(start, part), part)
            parts.append((columns, grad_ref, pl.ds(place * part, part)))

    def step(index, _):
        at = pl.ds(pl.multiple_of(index * ROWS, ROWS), ROWS)
        inverse = inverse_ref[at, :][:, :1]
        total = jnp.zeros((ROWS, 1), f32)
        for columns, grad_ref, place in parts:
            scaled = grad_ref[at, place].astype(f32) * scales_ref[:, columns]
            total += jnp.sum(scaled * hidden_ref[at, columns].astype(f32), axis=1, keepdims=True)
        shift = inverse * (inverse * total / width)
        for columns, grad_ref, place in parts:
            scaled = grad_ref[at, place].astype(f32) * scales_ref[:, columns]
            inner = scaled - hidden_ref[at, columns].astype(f32) * shift
            out_ref[at, columns] = (res_ref[at, columns].astype(f32) + inverse * inner).astype(bf16)
        return 0

    lax.fori_loop(0, tokens // ROWS, step, 0, unroll=2)


def gain_kernel(place_ref, grad_ref, weight_ref, scales_ref, gain_ref):
    rows = grad_ref.shape[0]
    products = weight_ref[...].astype(f32) * grad_ref[...].astype(f32)
    sums = lax.dot_general(
        jnp.ones((8, products.shape[1]), f32),
        products,
        (((1,), (1,)), ((), ())),
        precision=lax.Precision.HIGHEST,
        preferred_element_type=f32,
    )
    columns = pl.ds(pl.multiple_of(place_ref[0] * rows, rows), rows)
    gain_ref[...] = sums[:1, :] / scales_ref[:, columns]


def body(
    hidden_in, res_grad, value_grad, value_weight, norm_gain, inner_frag, outer_frag, momentum
):
    upper = lax.axis_index("x_hi").reshape(1)
    twist = lax.bitwise_xor(lax.axis_index("x_hi"), lax.axis_index("y_hi") // 2).reshape(1)
    own_weight = value_weight[0]
    tokens, width = hidden_in.shape
    half = width // 2
    weight_half = lax.all_gather(own_weight, FSDP, axis=0, tiled=True, axis_index_groups=TWISTED)
    partner_value = lax.ppermute(value_grad, "x_hi", SWAP)

    kept, sent, inverse = call(
        norm_kernel,
        (
            shape((tokens, half), bf16),
            shape((tokens, half), bf16),
            shape((tokens, 128), f32),
        ),
        (upper, hidden_in, norm_gain),
    )
    received = lax.ppermute(sent, "x_hi", SWAP)
    term = lax.dot_general(
        jnp.concatenate([kept, received], axis=0),
        jnp.concatenate([value_grad, partner_value], axis=0),
        (((0,), (0,)), ((), ())),
        preferred_element_type=f32,
    ).astype(bf16)
    weight_grad = lax.psum_scatter(
        term, ("y_hi", "y_lo"), scatter_dimension=0, tiled=True
    )

    rows, columns = outer_frag.shape
    split = (columns // 128, rows, 128)
    pseudo_grad = call(
        pseudo_kernel, shape(split, bf16), (outer_frag, inner_frag[0])
    ).reshape(48, -1, 128)
    spread = lax.all_to_all(pseudo_grad, REPLICA, 0, 0)
    block = call(block_kernel, shape(spread.shape, bf16), (spread,))
    shared = lax.all_to_all(block, REPLICA, 0, 0)
    new_outer, new_momentum = call(
        outer_kernel,
        (shape(outer_frag.shape, f32), shape(outer_frag.shape, f32)),
        (shared.reshape(split), outer_frag, momentum),
    )

    rows_by_rows = (((1,), (1,)), ((), ()))
    partner_grad = lax.dot_general(
        partner_value, weight_half, rows_by_rows, preferred_element_type=f32
    ).astype(bf16)
    other_grad = lax.ppermute(partner_grad, "x_hi", SWAP)
    own_grad = lax.dot_general(value_grad, weight_half, rows_by_rows, preferred_element_type=f32)
    hidden_grad = call(
        hidden_kernel,
        shape(hidden_in.shape, bf16),
        (twist, hidden_in, res_grad, norm_gain, inverse, own_grad, other_grad),
    )

    gain_grad = call(
        gain_kernel,
        shape((1, own_weight.shape[0]), f32),
        (lax.axis_index(FSDP).reshape(1), weight_grad, own_weight, norm_gain),
    )
    return (hidden_grad, weight_grad[None], gain_grad, new_outer, new_momentum)


def solution(mesh):
    grid = Mesh(mesh.devices.reshape(2, 12, 2, 2, 4, 2), AXES)
    in_specs = (
        P(AXES, None),
        P(AXES, None),
        P(AXES, None),
        P(REPLICA, FSDP, None),
        P(REPLICA, None),
        P(REPLICA, FSDP, None),
        P(FSDP, None),
        P(FSDP, None),
    )
    out_specs = (
        P(AXES, None),
        P(REPLICA, FSDP, None),
        P(REPLICA, FSDP),
        P(FSDP, None),
        P(FSDP, None),
    )

    def step(*arrays):
        return body(*arrays)

    step = jax.shard_map(step, mesh=grid, in_specs=in_specs, out_specs=out_specs, check_vma=False)
    return step
```
